32 devices in a mesh: groups: 2 (over x), gx: 4 (over y, core), gy: 4 (over z).
Axes of the slice: x: 2, y: 2, z: 4, core: 2. Of those that a mesh axis runs over, the one named last changes fastest.
Arguments:
- features: bfloat16 [8, 4, 4, 64, 256], P(('groups', 'gx'), 'gy'), parts along dimension 0, may hold values from -6 to 6
- neighbour_table: int32 [8, 4, 4, 27], P(('groups', 'gx'), 'gy'), parts along dimension 0, may hold values from 0 to 36, as said below
- kernel_weight: bfloat16 [27, 256, 256], replicated, may hold values from -0.078125 to 0.078125
- out_cotangent: bfloat16 [8, 4, 4, 64, 256], P(('groups', 'gx'), 'gy'), parts along dimension 0, may hold values from -6 to 6
Outputs:
- out_features: bfloat16 [8, 4, 4, 64, 256], P(('groups', 'gx'), 'gy'), parts along dimension 0
- grad_features: bfloat16 [8, 4, 4, 64, 256], P(('groups', 'gx'), 'gy'), parts along dimension 0
- grad_kernel: float32 [13824, 256], P(('groups', 'gx')), parts along dimension 0
The draws below stay inside these ranges and needn't reach their ends.
There are 2 independent parts, one for each index of `groups`. The reference program is written for one: setup_inputs(seed, part) draws one part's arguments, and reference() takes and returns one part's arrays. A program takes and returns all parts, laid end to end along the dimension named above; an argument that names none is the same for every part. Nothing has to cross between parts.
Inputs may be any that keep to these rules, and one draw needn't show every extreme that they name: `neighbour_table`: within a tile the live slots come first; an empty slot has all 27 entries equal to 36; a live slot s has entry 16 + s at offset 13; adjacency is symmetric; some tile has all 4 slots live and the live counts differ much between tiles.
All inputs are finite; a program needn't handle non-finite values.
Results may differ from the reference program's by a relative error of at most 0.001.
Values may be sent and summed in bfloat16 or wider, within the bound.
A program may use at most 128 MiB of HBM per device.

```python
import jax
import jax.numpy as jnp
from jax import lax

C = 256
VOX = 64
TB = 4
H = 2
BCAP = 4
TILES_X = 4
TILES_Y = 4


def draw_neighbour_table(key, part):
    tile_count = TILES_X * TILES_Y
    cell_count = TB * TB * H
    key_count, key_full, key_perm = jax.random.split(jax.random.fold_in(key, 11), 3)
    spread = jax.random.randint(key_count, (tile_count,), 0, 13)
    counts = 2 + spread * spread * (BCAP - 2) // 144
    full_tile = jax.random.randint(key_full, (), 0, tile_count)
    counts = jnp.where(jnp.arange(tile_count) == full_tile, BCAP, counts)
    orders = jax.vmap(lambda single_key: jax.random.permutation(single_key, cell_count))(jax.random.split(key_perm, tile_count))
    cell_ranks = jnp.argsort(orders, axis=1)
    slot_grid = jnp.where(cell_ranks < counts[:, None], cell_ranks, -1)
    slot_grid = slot_grid.reshape(TILES_X, TILES_Y, TB, TB, H).transpose(0, 2, 1, 3, 4).reshape(TILES_X * TB, TILES_Y * TB, H)
    live_cells = orders[:, :BCAP]
    live_slot = jnp.arange(BCAP)[None, :] < counts[:, None]
    cell_x = live_cells // (TB * H)
    cell_y = live_cells // H % TB
    cell_z = live_cells % H
    tile_x = (jnp.arange(tile_count) // TILES_Y)[:, None]
    tile_y = (jnp.arange(tile_count) % TILES_Y)[:, None]
    place_x = tile_x * TB + cell_x
    place_y = tile_y * TB + cell_y
    columns = []
    for step_x in (-1, 0, 1):
        for step_y in (-1, 0, 1):
            for step_z in (-1, 0, 1):
                near_x = place_x + step_x
                near_y = place_y + step_y
                near_z = cell_z + step_z
                inside = (near_x >= 0) & (near_x < TILES_X * TB) & (near_y >= 0) & (near_y < TILES_Y * TB) & (near_z >= 0) & (near_z < H)
                found = slot_grid[jnp.clip(near_x, 0, TILES_X * TB - 1), jnp.clip(near_y, 0, TILES_Y * TB - 1), jnp.clip(near_z, 0, H - 1)]
                block_index = (jnp.floor_divide(near_x, TB) - tile_x + 1) * 3 + (jnp.floor_divide(near_y, TB) - tile_y + 1)
                usable = inside & (found >= 0) & live_slot
                columns.append(jnp.where(usable, block_index * BCAP + found, 9 * BCAP))
    brick_table = jnp.stack(columns, axis=-1).reshape(TILES_X, TILES_Y, BCAP, 27)
    return brick_table.astype(jnp.int32)


def block_levels(key, dims, pieces, smallest, top_value):
    def one(position, shards_of):
        draws = jax.random.uniform(jax.random.fold_in(jax.random.fold_in(key, 6), position), (shards_of,), jnp.float32, smallest / len(pieces), top_value / len(pieces))
        return jnp.repeat(jnp.exp(draws), dims[position] // shards_of).reshape((-1,) + (1,) * (len(dims) - position - 1))

    loudness = one(*pieces[0])
    for cut in pieces[1:]:
        loudness = loudness * one(*cut)
    return loudness


def scatter_about(key, dims, scale, most, pieces=(), kind=jnp.bfloat16):
    values = jax.random.normal(key, dims, jnp.float32) * scale
    if len(pieces) > 0:
        values = block_levels(key, dims, pieces, -0.22, 0.18) * values
    return jnp.clip(values, min=-most, max=most).astype(kind)


def setup_inputs(seed: int = 0, part: int = 0) -> dict:
    key_list = jax.random.split(jax.random.key(seed), 5)
    part_keys = jax.random.split(jax.random.fold_in(key_list[4], part), 5)
    return {
        "features": scatter_about(part_keys[0], (TILES_X, TILES_Y, BCAP, VOX, C), 1.0, 6.0, ((0, 4), (1, 4))),
        "neighbour_table": draw_neighbour_table(jax.random.fold_in(jax.random.fold_in(key_list[4], part), 71), part),
        "kernel_weight": scatter_about(key_list[2], (27, C, C), (27 * C) ** -0.5, 0.078125),
        "out_cotangent": scatter_about(part_keys[3], (TILES_X, TILES_Y, BCAP, VOX, C), 1.0, 6.0, ((0, 4), (1, 4))),
    }


kernel_scale = 0.00390625
offset_list = [(first_step, second_step, third_step) for first_step in (-1, 0, 1) for second_step in (-1, 0, 1) for third_step in (-1, 0, 1)]
source_spans = ((3, 4), (0, 4), (0, 1))
target_spans = ((0, 1), (1, 5), (5, 6))


def assemble_block(extended, brick_table):
    slot_total = brick_table.shape[0]
    channels = extended.shape[-1]
    bricks = extended.reshape(extended.shape[0], 4, 4, 4, channels)
    padded = jnp.zeros((slot_total, 6, 6, 6, channels), extended.dtype)
    for offset_index, shift in enumerate(offset_list):
        brick_piece = jnp.take(bricks, brick_table[:, offset_index].astype(jnp.int32), axis=0)
        source_x, source_y, source_z = [source_spans[value + 1] for value in shift]
        target_x, target_y, target_z = [target_spans[value + 1] for value in shift]
        brick_piece = brick_piece[:, source_x[0]:source_x[1], source_y[0]:source_y[1], source_z[0]:source_z[1], :]
        padded = padded.at[:, target_x[0]:target_x[1], target_y[0]:target_y[1], target_z[0]:target_z[1], :].set(brick_piece)
    return padded


def window(padded, shift, sign):
    channels = padded.shape[-1]
    lower = [1 + sign * value for value in shift]
    return padded[:, lower[0]:lower[0] + 4, lower[1]:lower[1] + 4, lower[2]:lower[2] + 4, :].reshape(-1, channels)


def forward_conv(padded, kernel_weight):
    summed = None
    for offset_index, shift in enumerate(offset_list):
        product = jnp.dot(window(padded, shift, 1), kernel_weight[offset_index], preferred_element_type=jnp.float32)
        summed = product if summed is None else summed + product
    return summed


def pull_conv(cot_padded, kernel_weight):
    summed = None
    for offset_index, shift in enumerate(offset_list):
        product = lax.dot_general(window(cot_padded, shift, -1), kernel_weight[offset_index], (((1,), (1,)), ((), ())), preferred_element_type=jnp.float32)
        summed = product if summed is None else summed + product
    return summed


def kernel_term(padded, cot_flat):
    blocks_list = []
    for offset_index, shift in enumerate(offset_list):
        blocks_list.append(lax.dot_general(window(padded, shift, 1), cot_flat, (((0,), (0,)), ((), ())), preferred_element_type=jnp.float32))
    return jnp.concatenate(blocks_list, axis=0) * kernel_scale


def widen_tiles(values):
    padded_tiles = jnp.pad(values, ((1, 1), (1, 1), (0, 0), (0, 0), (0, 0)))
    flat = padded_tiles.reshape(-1, values.shape[3], values.shape[4])
    return jnp.concatenate([flat, jnp.zeros((1, values.shape[3], values.shape[4]), values.dtype)], axis=0)


def reference(features, neighbour_table, kernel_weight, out_cotangent):
    tiles_x, tiles_y, slot_count, voxels, channels = features.shape
    extended = widen_tiles(features)
    cot_extended = widen_tiles(out_cotangent)
    zero_index = extended.shape[0] - 1
    tile_row = jnp.arange(tiles_x, dtype=jnp.int32)[:, None, None, None]
    tile_col = jnp.arange(tiles_y, dtype=jnp.int32)[None, :, None, None]
    block_index = neighbour_table // slot_count
    slot_index = neighbour_table % slot_count
    global_table = ((tile_row + block_index // 3) * (tiles_y + 2) + (tile_col + block_index % 3)) * slot_count + slot_index
    global_table = jnp.where(neighbour_table == 9 * slot_count, zero_index, global_table).astype(jnp.int32)

    def per_row(running, row_items):
        row_table, row_cot = row_items
        flat_table = row_table.reshape(-1, 27)
        padded = assemble_block(extended, flat_table)
        out_row = forward_conv(padded, kernel_weight).astype(jnp.bfloat16)
        cot_padded = assemble_block(cot_extended, flat_table)
        grad_row = pull_conv(cot_padded, kernel_weight).astype(jnp.bfloat16)
        running = running + kernel_term(padded, row_cot.reshape(-1, channels))
        return running, (out_row, grad_row)

    initial = jnp.zeros((27 * channels, channels), jnp.float32)
    grad_kernel, (out_rows, grad_rows) = lax.scan(per_row, initial, (global_table, out_cotangent))
    return out_rows.reshape(features.shape), grad_rows.reshape(features.shape), grad_kernel
```

```python
import functools

import jax
import jax.numpy as jnp
import numpy as np
from jax import lax
from jax.experimental import pallas as pl
from jax.experimental.pallas import tpu as pltpu
from jax.sharding import PartitionSpec as P

kernel_scale = 0.00390625
slots = 4
rows = 64
channels = 256
MESH = pl.DeviceIdType.MESH


def shift_matrix():
    out = np.zeros((9, 4, 4, 9, 4, 4), np.float32)
    for b in (-1, 0, 1):
        for c in (-1, 0, 1):
            for y in range(4):
                for z in range(4):
                    source = ((y + b) // 4 + 1) * 3 + (z + c) // 4 + 1
                    out[(b + 1) * 3 + c + 1, y, z, source, (y + b) % 4, (z + c) % 4] = 1
    return jnp.asarray(out.reshape(144, 144), jnp.bfloat16)


def ring_place(position, chips_y, chips_z):
    inner = chips_y * (chips_z - 1)
    y_in = position // (chips_z - 1)
    step = position % (chips_z - 1)
    z_in = jnp.where(y_in % 2 == 0, 1 + step, chips_z - 1 - step)
    on_edge = position >= inner
    y = jnp.where(on_edge, chips_y - 1 - (position - inner), y_in)
    z = jnp.where(on_edge, 0, z_in)
    return y, z


def ring_position(y, z, chips_y, chips_z):
    inside = y * (chips_z - 1) + jnp.where(y % 2 == 0, z - 1, chips_z - 1 - z)
    return jnp.where(z == 0, chips_y * (chips_z - 1) + chips_y - 1 - y, inside)


def gather_kernel(chips_y, chips_z, *refs):
    sources = refs[0:3]
    targets = refs[3:6]
    own_sem, ring_send, ring_recv, pair_send, pair_recv = refs[6:]
    count = chips_y * chips_z
    half = count // 2
    gx = lax.axis_index("gx")
    z = lax.axis_index("gy")
    y = gx // 2
    core = gx % 2
    here = ring_position(y, z, chips_y, chips_z)

    def place(step):
        return ring_place((here + step + count) % count, chips_y, chips_z)

    def tile(step, which):
        ty, tz = place(step)
        return (ty * 2 + which) * chips_z + tz

    def device(step):
        ty, tz = place(step)
        return {"gx": ty * 2 + core, "gy": tz}

    partner = {"gx": y * 2 + 1 - core, "gy": z}
    near = (device(1), device(-1), partner)
    barrier = pltpu.get_barrier_semaphore()
    for peer in near:
        pl.semaphore_signal(barrier, inc=1, device_id=peer, device_id_type=MESH)

    def ring_copy(array, side, step):
        index = tile((1 - step) if side == 0 else (step - 1), core)
        src = sources[array].at[0] if step == 1 else targets[array].at[index]
        return pltpu.make_async_remote_copy(
            src_ref=src,
            dst_ref=targets[array].at[index],
            send_sem=ring_send.at[array, side, step - 1],
            recv_sem=ring_recv.at[array, side, step - 1],
            device_id=device(1) if side == 0 else device(-1),
            device_id_type=MESH,
        )

    def ring_wait(array, side, step):
        index = tile(-step if side == 0 else step, core)
        pltpu.make_async_remote_copy(
            src_ref=targets[array].at[index],
            dst_ref=targets[array].at[index],
            send_sem=ring_send.at[array, side, step - 1],
            recv_sem=ring_recv.at[array, side, step - 1],
            device_id=device(1),
            device_id_type=MESH,
        ).wait_recv()

    def pair_copy(array, step, which):
        number = step % count
        index = tile(step, which)
        src = sources[array].at[0] if step == 0 else targets[array].at[index]
        return pltpu.make_async_remote_copy(
            src_ref=src,
            dst_ref=targets[array].at[index],
            send_sem=pair_send.at[array, number],
            recv_sem=pair_recv.at[array, number],
            device_id=partner,
            device_id_type=MESH,
        )

    def reach(array, side):
        return half if (array % 2) == side else half - 1

    own = []
    for array in range(3):
        copy = pltpu.make_async_copy(
            sources[array].at[0], targets[array].at[tile(0, core)], own_sem.at[array]
        )
        copy.start()
        own.append(copy)
    pl.semaphore_wait(barrier, 3)
    started = []
    for step in range(1, half + 2):
        for array in range(3):
            for side in (0, 1):
                if step - 1 > reach(array, side):
                    continue
                if step > 1:
                    ring_wait(array, side, step - 1)
                if step <= reach(array, side):
                    copy = ring_copy(array, side, step)
                    copy.start()
                    started.append(copy)
                if step > 1:
                    copy = pair_copy(array, (1 - step) if side == 0 else (step - 1), core)
                    copy.start()
                    started.append(copy)
            if step == 1:
                copy = pair_copy(array, 0, core)
                copy.start()
                started.append(copy)
    for array in range(3):
        own[array].wait()
        for number in range(count):
            pair_copy(array, number, 1 - core).wait_recv()
    for copy in started:
        copy.wait_send()


def gather_tiles(table, cot, features, chips_y, chips_z):
    count = chips_y * chips_z
    tiles = 2 * count
    arrays = (table, cot, features)
    return pl.pallas_call(
        functools.partial(gather_kernel, chips_y, chips_z),
        out_shape=[jax.ShapeDtypeStruct((tiles,) + a.shape[1:], a.dtype) for a in arrays],
        in_specs=[pl.BlockSpec(memory_space=pltpu.VMEM)] * 3,
        out_specs=[pl.BlockSpec(memory_space=pl.ANY)] * 3,
        scratch_shapes=[
            pltpu.SemaphoreType.DMA((3,)),
            pltpu.SemaphoreType.DMA((3, 2, count // 2)),
            pltpu.SemaphoreType.DMA((3, 2, count // 2)),
            pltpu.SemaphoreType.DMA((3, count)),
            pltpu.SemaphoreType.DMA((3, count)),
        ],
        compiler_params=pltpu.CompilerParams(collective_id=0, has_side_effects=True),
        name="gather_tiles",
    )(*arrays)


def conv_kernel(bricks, part_rows, picked, gy_size, *refs):
    (table, shifts, cot_hbm, feat_hbm, weight_hbm, out_ref, grad_ref, term_hbm) = refs[:8]
    (cot, feat, weight, near, total, flat, order, sems) = refs[8:]
    gx = lax.axis_index("gx")
    gy = lax.axis_index("gy")
    copies = (
        pltpu.make_async_copy(cot_hbm, cot.at[pl.ds(0, bricks)], sems.at[0]),
        pltpu.make_async_copy(feat_hbm, feat.at[pl.ds(0, bricks)], sems.at[1]),
        pltpu.make_async_copy(weight_hbm, weight, sems.at[2]),
    )
    for copy in copies:
        copy.start()
    cot[bricks] = jnp.zeros((rows, channels), jnp.bfloat16)
    feat[bricks] = jnp.zeros((rows, channels), jnp.bfloat16)
    total[...] = jnp.zeros_like(total)

    def entry(brick, offset):
        return table[brick // slots, (brick % slots) * 32 + offset]

    def count_live(brick, found):
        @pl.when(entry(brick, 13) != bricks)
        def _():
            order[found] = brick

        return found + (entry(brick, 13) != bricks).astype(jnp.int32)

    live = lax.fori_loop(0, bricks, count_live, jnp.int32(0))
    for extra in range(slots):
        order[live + extra] = 0

    def surround(source, slot, brick, valid):
        names = []
        for offset in range(27):
            name = entry(brick, offset)
            names.append(name if valid is None else jnp.where(valid, name, bricks))
        for x in range(6):
            side = 0 if x == 0 else (2 if x == 5 else 1)
            plane = (x + 3) % 4
            stack = jnp.concatenate(
                [source[names[side * 9 + n], plane * 16 : plane * 16 + 16, :] for n in range(9)],
                axis=0,
            )
            moved = jnp.dot(shifts[...], stack, preferred_element_type=jnp.float32)
            near[:, slot, x] = moved.astype(jnp.bfloat16).reshape(9, 16, channels)

    def window(a, b, c):
        return near[(b + 1) * 3 + c + 1, :, pl.ds(1 + a, 4)].reshape(slots * rows, channels)

    first = (gx * part_rows) // channels
    for copy in copies[:2]:
        copy.wait()

    def group(number, carry):
        names = []
        for slot in range(slots):
            place = number * slots + slot
            brick = order[place]
            valid = place < live
            surround(cot, slot, brick, valid)
            names.append(brick)
        block = jnp.concatenate([feat[name] for name in names], axis=0).T

        def one(n, inner):
            offset = jnp.minimum(first + n, 26)
            a = offset // 9 - 1
            b = (offset // 3) % 3 - 1
            c = offset % 3 - 1
            at = pl.multiple_of(n * channels, channels)
            total[pl.ds(at, channels), :] += jnp.dot(
                block, window(-a, -b, -c), preferred_element_type=jnp.float32
            )
            return inner

        return lax.fori_loop(0, picked, one, carry, unroll=True)

    lax.fori_loop(0, (live + slots - 1) // slots, group, 0)
    start = pl.multiple_of(gx * part_rows - first * channels, 8)
    span = pl.ds(start, part_rows)
    total[span, :] = total[span, :] * kernel_scale
    result = pltpu.make_async_copy(total.at[span], term_hbm, sems.at[3])
    result.start()
    copies[2].wait()
    mine = (gx * gy_size + gy) * slots
    for sign, source, target in ((-1, cot, grad_ref), (1, feat, out_ref)):
        for slot in range(slots):
            surround(source, slot, mine + slot, None)
        for offset in range(27):
            a, b, c = offset // 9 - 1, (offset // 3) % 3 - 1, offset % 3 - 1
            dims = (((1,), (0 if sign == 1 else 1,)), ((), ()))
            product = lax.dot_general(
                window(sign * a, sign * b, sign * c),
                weight[offset],
                dims,
                preferred_element_type=jnp.float32,
            )
            if offset == 0:
                flat[...] = product
            elif offset < 26:
                flat[...] += product
            else:
                target[...] = (flat[...] + product).astype(jnp.bfloat16)
    result.wait()


def convolve(table_all, cot_all, feat_all, kernel_weight, part_rows, picked, gy_size):
    bricks = cot_all.shape[0]
    own = (slots * rows, channels)
    whole = pl.BlockSpec(memory_space=pltpu.VMEM)
    far = pl.BlockSpec(memory_space=pl.ANY)
    return pl.pallas_call(
        functools.partial(conv_kernel, bricks, part_rows, picked, gy_size),
        out_shape=[
            jax.ShapeDtypeStruct(own, jnp.bfloat16),
            jax.ShapeDtypeStruct(own, jnp.bfloat16),
            jax.ShapeDtypeStruct((part_rows, channels), jnp.float32),
        ],
        in_specs=[pl.BlockSpec(memory_space=pltpu.SMEM), whole, far, far, far],
        out_specs=[whole, whole, far],
        scratch_shapes=[
            pltpu.VMEM((bricks + 1, rows, channels), jnp.bfloat16),
            pltpu.VMEM((bricks + 1, rows, channels), jnp.bfloat16),
            pltpu.VMEM(kernel_weight.shape, jnp.bfloat16),
            pltpu.VMEM((9, slots, 6, 16, channels), jnp.bfloat16),
            pltpu.VMEM((picked * channels, channels), jnp.float32),
            pltpu.VMEM(own, jnp.float32),
            pltpu.SMEM((bricks + slots,), jnp.int32),
            pltpu.SemaphoreType.DMA((4,)),
        ],
        compiler_params=pltpu.CompilerParams(vmem_limit_bytes=62 * 2**20),
        name="convolve",
    )(table_all, shift_matrix(), cot_all, feat_all, kernel_weight)


def body(gx_size, gy_size, features, neighbour_table, kernel_weight, out_cotangent):
    gx = lax.axis_index("gx")
    gy = lax.axis_index("gy")
    tiles = gx_size * gy_size
    bricks = tiles * slots
    table = neighbour_table[0, 0]
    block = table // slots
    owner = (gx + block // 3 - 1) * gy_size + gy + block % 3 - 1
    named = jnp.where(table == 9 * slots, bricks, owner * slots + table % slots)
    named = jnp.pad(named, ((0, 0), (0, 5))).reshape(1, 1, 128)
    flat = (1, slots, rows, channels)
    table_all, cot_all, feat_all = gather_tiles(
        named, out_cotangent.reshape(flat), features.reshape(flat), gx_size // 2, gy_size
    )
    part_rows = 27 * channels // gx_size
    picked = max(
        -(-((g + 1) * part_rows) // channels) - g * part_rows // channels for g in range(gx_size)
    )
    out, grad, term = convolve(
        table_all.reshape(tiles, 128),
        cot_all.reshape(bricks, rows, channels),
        feat_all.reshape(bricks, rows, channels),
        kernel_weight,
        part_rows,
        picked,
        gy_size,
    )
    return out.reshape(features.shape), grad.reshape(features.shape), term


def solution(mesh):
    in_specs = (
        P(("groups", "gx"), "gy", None, None, None),
        P(("groups", "gx"), "gy", None, None),
        P(),
        P(("groups", "gx"), "gy", None, None, None),
    )
    out_specs = (
        P(("groups", "gx"), "gy", None, None, None),
        P(("groups", "gx"), "gy", None, None, None),
        P(("groups", "gx"), None),
    )
    return jax.shard_map(
        functools.partial(body, mesh.shape["gx"], mesh.shape["gy"]),
        mesh=mesh,
        in_specs=in_specs,
        out_specs=out_specs,
        check_vma=False,
    )
```

```python
import functools

import jax
import jax.numpy as jnp
import numpy as np
from jax import lax
from jax.experimental import pallas as pl
from jax.experimental.pallas import tpu as pltpu
from jax.sharding import PartitionSpec as P

kernel_scale = 0.00390625
slots = 4
rows = 64
channels = 256
MESH = pl.DeviceIdType.MESH


def shift_matrix():
    out = np.zeros((9, 4, 4, 9, 4, 4), np.float32)
    for b in (-1, 0, 1):
        for c in (-1, 0, 1):
            for y in range(4):
                for z in range(4):
                    source = ((y + b) // 4 + 1) * 3 + (z + c) // 4 + 1
                    out[(b + 1) * 3 + c + 1, y, z, source, (y + b) % 4, (z + c) % 4] = 1
    return jnp.asarray(out.reshape(144, 144), jnp.bfloat16)


def ring_place(position, chips_y, chips_z):
    inner = chips_y * (chips_z - 1)
    y_in = position // (chips_z - 1)
    step = position % (chips_z - 1)
    z_in = jnp.where(y_in % 2 == 0, 1 + step, chips_z - 1 - step)
    on_edge = position >= inner
    y = jnp.where(on_edge, chips_y - 1 - (position - inner), y_in)
    z = jnp.where(on_edge, 0, z_in)
    return y, z


def ring_position(y, z, chips_y, chips_z):
    inside = y * (chips_z - 1) + jnp.where(y % 2 == 0, z - 1, chips_z - 1 - z)
    return jnp.where(z == 0, chips_y * (chips_z - 1) + chips_y - 1 - y, inside)


def fused_kernel(chips_y, chips_z, part_rows, picked, early, *refs):
    (table_ref, cot_ref, feat_ref, shifts, weight_hbm, out_ref, grad_ref, term_hbm) = refs[:8]
    (table_all, table, cot, feat, weight, around, near, total, flat) = refs[8:17]
    local_sem, ring_send, ring_recv, pair_send, pair_recv = refs[17:]
    count = chips_y * chips_z
    half = count // 2
    tiles = 2 * count
    bricks = tiles * slots
    gx = lax.axis_index("gx")
    z = lax.axis_index("gy")
    y = gx // 2
    core = gx % 2
    here = ring_position(y, z, chips_y, chips_z)

    def place(step):
        return ring_place((here + step + count) % count, chips_y, chips_z)

    def tile(step, which):
        ty, tz = place(step)
        return (ty * 2 + which) * chips_z + tz

    def device(step):
        ty, tz = place(step)
        return {"gx": ty * 2 + core, "gy": tz}

    partner = {"gx": y * 2 + 1 - core, "gy": z}
    right, left = device(1), device(-1)
    barrier = pltpu.get_barrier_semaphore()
    for peer in (right, left, partner):
        pl.semaphore_signal(barrier, inc=1, device_id=peer, device_id_type=MESH)

    def landing(stream, index):
        if stream == 0:
            return table_all.at[index]
        target = cot if stream < 3 else feat
        return target.at[pl.ds(index * slots + (stream + 1) % 2 * 2, 2)]

    def origin(stream):
        if stream == 0:
            return table_ref.at[0]
        target = cot_ref if stream < 3 else feat_ref
        return target.at[pl.ds((stream + 1) % 2 * 2, 2)]

    def ring_copy(stream, side, step):
        index = tile((1 - step) if side == 0 else (step - 1), core)
        return pltpu.make_async_remote_copy(
            src_ref=origin(stream) if step == 1 else landing(stream, index),
            dst_ref=landing(stream, index),
            send_sem=ring_send.at[stream, side, step - 1],
            recv_sem=ring_recv.at[stream, side, step - 1],
            device_id=right if side == 0 else left,
            device_id_type=MESH,
        )

    def ring_wait(stream, side, step):
        index = tile(-step if side == 0 else step, core)
        pltpu.make_async_remote_copy(
            src_ref=landing(stream, index),
            dst_ref=landing(stream, index),
            send_sem=ring_send.at[stream, side, step - 1],
            recv_sem=ring_recv.at[stream, side, step - 1],
            device_id=right,
            device_id_type=MESH,
        ).wait_recv()

    def pair_copy(stream, step, which):
        number = step % count
        index = tile(step, which)
        return pltpu.make_async_remote_copy(
            src_ref=origin(stream) if step == 0 else landing(stream, index),
            dst_ref=landing(stream, index),
            send_sem=pair_send.at[stream, number],
            recv_sem=pair_recv.at[stream, number],
            device_id=partner,
            device_id_type=MESH,
        )

    def reach(stream, side):
        return half if (stream % 2) == side else half - 1

    started = []

    def launch(copy):
        copy.start()
        started.append(copy)

    def advance(streams, step):
        for stream in streams:
            for side in (0, 1):
                if step - 1 > reach(stream, side):
                    continue
                if step > 1:
                    ring_wait(stream, side, step - 1)
                if step <= reach(stream, side):
                    launch(ring_copy(stream, side, step))
                if step > 1:
                    launch(pair_copy(stream, (1 - step) if side == 0 else (step - 1), core))
            if step == 1:
                launch(pair_copy(stream, 0, core))

    def settle(streams):
        for stream in streams:
            for number in range(count):
                pair_copy(stream, number, 1 - core).wait_recv()

    weight_copy = pltpu.make_async_copy(weight_hbm, weight, local_sem.at[0])
    weight_copy.start()
    mine = gx * chips_z + z
    cot[pl.ds(mine * slots, slots)] = cot_ref[...]
    feat[pl.ds(mine * slots, slots)] = feat_ref[...]
    table_all[mine] = table_ref[0]
    cot[bricks] = jnp.zeros((rows, channels), jnp.bfloat16)
    feat[bricks] = jnp.zeros((rows, channels), jnp.bfloat16)
    total[...] = jnp.zeros_like(total)
    pl.semaphore_wait(barrier, 3)

    early_streams, late_streams = (0, 1, 2), (3, 4)
    for step in range(1, half + 1):
        advance(early_streams, step)
    advance(late_streams, 1)
    advance(early_streams, half + 1)
    settle(early_streams)
    table_copy = pltpu.make_async_copy(table_all, table, local_sem.at[1])
    table_copy.start()
    table_copy.wait()

    def entry(brick, offset):
        return table[brick // slots, 0, (brick % slots) * 32 + offset]

    first = (gx * part_rows) // channels
    last = jnp.minimum(first + picked - 1, 26)
    lowest = jnp.minimum(2 - last // 9, 1)

    def surround(source, brick, x, store):
        side = (x + 3) // 4
        plane = pl.multiple_of((x + 3) % 4 * 16, 16)
        planes = [
            source[entry(brick, side * 9 + n), pl.ds(plane, 16), :] for n in range(9)
        ]
        moved = jnp.dot(
            shifts[...], jnp.concatenate(planes, axis=0), preferred_element_type=jnp.float32
        )
        store(moved.astype(jnp.bfloat16).reshape(9, 16, channels))

    def build(number, carry):
        slab = number if early else 0
        for slot in range(slots):
            for x in range(5):

                def store(value):
                    around[slab, :, slot, x] = value

                surround(cot, number * slots + slot, lowest + x, store)
        return carry

    def gather_term(number, carry):
        slab = number if early else 0
        if not early:
            build(number, carry)
        at = pl.multiple_of(number * slots, slots)
        block = feat[pl.ds(at, slots)].reshape(slots * rows, channels).T
        for n in range(picked):
            offset = jnp.minimum(first + n, 26)
            a = offset // 9 - 1
            b = (offset // 3) % 3 - 1
            c = offset % 3 - 1
            seen = around[slab, (1 - b) * 3 + 1 - c, :, pl.ds(1 - a - lowest, 4)]
            total[n * channels : (n + 1) * channels, :] += jnp.dot(
                block,
                seen.reshape(slots * rows, channels),
                preferred_element_type=jnp.float32,
            )
        return carry

    def own_conv(sign, source, target):
        def gather_slot(slot, carry):
            for x in range(6):

                def store(value):
                    near[:, slot, x] = value

                surround(source, mine * slots + slot, x, store)
            return carry

        lax.fori_loop(0, slots, gather_slot, 0)
        flat[...] = jnp.zeros_like(flat)

        def one(bc, carry):
            here_bc = bc if sign == 1 else 8 - bc
            product = None
            for a in range(3):
                seen = near[here_bc, :, (a if sign == 1 else 2 - a) : (a if sign == 1 else 2 - a) + 4]
                part = lax.dot_general(
                    seen.reshape(slots * rows, channels),
                    weight[a * 9 + bc],
                    (((1,), (0 if sign == 1 else 1,)), ((), ())),
                    preferred_element_type=jnp.float32,
                )
                product = part if product is None else product + part
            flat[...] += product
            return carry

        lax.fori_loop(0, 9, one, 0)
        target[...] = flat[...].astype(jnp.bfloat16)

    done = 0
    for step in range(2, half + 2):
        if early:
            until = tiles * (step - 1) // half
            lax.fori_loop(done, until, build, 0)
            done = until
        if step == half + 1:
            weight_copy.wait()
            own_conv(-1, cot, grad_ref)
        advance(late_streams, step)
    settle(late_streams)
    lax.fori_loop(0, tiles, gather_term, 0)
    start = pl.multiple_of(gx * part_rows - first * channels, 8)
    span = pl.ds(start, part_rows)
    total[span, :] = total[span, :] * kernel_scale
    result = pltpu.make_async_copy(total.at[span], term_hbm, local_sem.at[2])
    result.start()
    own_conv(1, feat, out_ref)
    result.wait()
    for copy in started:
        copy.wait_send()


def convolve(table, cot, features, kernel_weight, part_rows, picked, chips_y, chips_z):
    count = chips_y * chips_z
    tiles = 2 * count
    bricks = tiles * slots
    own = (slots * rows, channels)
    plane = (16, channels)
    early = tiles <= 16
    whole = pl.BlockSpec(memory_space=pltpu.VMEM)
    far = pl.BlockSpec(memory_space=pl.ANY)
    return pl.pallas_call(
        functools.partial(fused_kernel, chips_y, chips_z, part_rows, picked, early),
        out_shape=[
            jax.ShapeDtypeStruct(own, jnp.bfloat16),
            jax.ShapeDtypeStruct(own, jnp.bfloat16),
            jax.ShapeDtypeStruct((part_rows, channels), jnp.float32),
        ],
        in_specs=[whole, whole, whole, whole, far],
        out_specs=[whole, whole, far],
        scratch_shapes=[
            pltpu.VMEM((tiles, 1, 128), jnp.int32),
            pltpu.SMEM((tiles, 1, 128), jnp.int32),
            pltpu.VMEM((bricks + 1, rows, channels), jnp.bfloat16),
            pltpu.VMEM((bricks + 1, rows, channels), jnp.bfloat16),
            pltpu.VMEM(kernel_weight.shape, jnp.bfloat16),
            pltpu.VMEM((tiles if early else 1, 9, slots, 5) + plane, jnp.bfloat16),
            pltpu.VMEM((9, slots, 6) + plane, jnp.bfloat16),
            pltpu.VMEM((picked * channels, channels), jnp.float32),
            pltpu.VMEM(own, jnp.float32),
            pltpu.SemaphoreType.DMA((3,)),
            pltpu.SemaphoreType.DMA((5, 2, count // 2)),
            pltpu.SemaphoreType.DMA((5, 2, count // 2)),
            pltpu.SemaphoreType.DMA((5, count)),
            pltpu.SemaphoreType.DMA((5, count)),
        ],
        compiler_params=pltpu.CompilerParams(
            collective_id=0, has_side_effects=True, vmem_limit_bytes=62 * 2**20
        ),
        name="convolve",
    )(table, cot, features, shift_matrix(), kernel_weight)


def body(gx_size, gy_size, features, neighbour_table, kernel_weight, out_cotangent):
    gx = lax.axis_index("gx")
    gy = lax.axis_index("gy")
    tiles = gx_size * gy_size
    bricks = tiles * slots
    table = neighbour_table[0, 0]
    block = table // slots
    owner = (gx + block // 3 - 1) * gy_size + gy + block % 3 - 1
    named = jnp.where(table == 9 * slots, bricks, owner * slots + table % slots)
    named = jnp.pad(named, ((0, 0), (0, 5))).reshape(1, 1, 128)
    part_rows = 27 * channels // gx_size
    picked = max(
        -(-((g + 1) * part_rows) // channels) - g * part_rows // channels for g in range(gx_size)
    )
    flat = (slots, rows, channels)
    out, grad, term = convolve(
        named,
        out_cotangent.reshape(flat),
        features.reshape(flat),
        kernel_weight,
        part_rows,
        picked,
        gx_size // 2,
        gy_size,
    )
    return out.reshape(features.shape), grad.reshape(features.shape), term


def solution(mesh):
    in_specs = (
        P(("groups", "gx"), "gy", None, None, None),
        P(("groups", "gx"), "gy", None, None),
        P(),
        P(("groups", "gx"), "gy", None, None, None),
    )
    out_specs = (
        P(("groups", "gx"), "gy", None, None, None),
        P(("groups", "gx"), "gy", None, None, None),
        P(("groups", "gx"), None),
    )
    return jax.shard_map(
        functools.partial(body, mesh.shape["gx"], mesh.shape["gy"]),
        mesh=mesh,
        in_specs=in_specs,
        out_specs=out_specs,
        check_vma=False,
    )
```

```python
import functools

import jax
import jax.numpy as jnp
import numpy as np
from jax import lax
from jax.experimental import pallas as pl
from jax.experimental.pallas import tpu as pltpu
from jax.sharding import PartitionSpec as P

kernel_scale = 0.00390625
slots = 4
rows = 64
channels = 256
MESH = pl.DeviceIdType.MESH


def shift_matrix():
    out = np.zeros((9, 4, 4, 9, 4, 4), np.float32)
    for b in (-1, 0, 1):
        for c in (-1, 0, 1):
            for y in range(4):
                for z in range(4):
                    source = ((y + b) // 4 + 1) * 3 + (z + c) // 4 + 1
                    out[(b + 1) * 3 + c + 1, y, z, source, (y + b) % 4, (z + c) % 4] = 1
    return jnp.asarray(out.reshape(144, 144), jnp.bfloat16)


def ring_place(position, chips_y, chips_z):
    inner = chips_y * (chips_z - 1)
    y_in = position // (chips_z - 1)
    step = position % (chips_z - 1)
    z_in = jnp.where(y_in % 2 == 0, 1 + step, chips_z - 1 - step)
    on_edge = position >= inner
    y = jnp.where(on_edge, chips_y - 1 - (position - inner), y_in)
    z = jnp.where(on_edge, 0, z_in)
    return y, z


def ring_position(y, z, chips_y, chips_z):
    inside = y * (chips_z - 1) + jnp.where(y % 2 == 0, z - 1, chips_z - 1 - z)
    return jnp.where(z == 0, chips_y * (chips_z - 1) + chips_y - 1 - y, inside)


def gather_kernel(chips_y, chips_z, *refs):
    sources = refs[0:3]
    targets = refs[3:6]
    ring_send, ring_recv, pair_send, pair_recv = refs[6:]
    count = chips_y * chips_z
    half = count // 2
    gx = lax.axis_index("gx")
    z = lax.axis_index("gy")
    y = gx // 2
    core = gx % 2
    here = ring_position(y, z, chips_y, chips_z)

    def place(step):
        return ring_place((here + step + count) % count, chips_y, chips_z)

    def landing(stream, index):
        if stream == 0:
            return targets[0].at[index]
        return targets[(stream + 1) // 2].at[pl.ds(index * slots + (stream + 1) % 2 * 2, 2)]

    def origin(stream):
        if stream == 0:
            return sources[0].at[0]
        return sources[(stream + 1) // 2].at[pl.ds((stream + 1) % 2 * 2, 2)]

    def tile(step, which):
        ty, tz = place(step)
        return (ty * 2 + which) * chips_z + tz

    def device(step):
        ty, tz = place(step)
        return {"gx": ty * 2 + core, "gy": tz}

    partner = {"gx": y * 2 + 1 - core, "gy": z}
    near = (device(1), device(-1), partner)
    barrier = pltpu.get_barrier_semaphore()
    for peer in near:
        pl.semaphore_signal(barrier, inc=1, device_id=peer, device_id_type=MESH)

    def ring_copy(array, side, step):
        index = tile((1 - step) if side == 0 else (step - 1), core)
        src = origin(array) if step == 1 else landing(array, index)
        return pltpu.make_async_remote_copy(
            src_ref=src,
            dst_ref=landing(array, index),
            send_sem=ring_send.at[array, side, step - 1],
            recv_sem=ring_recv.at[array, side, step - 1],
            device_id=device(1) if side == 0 else device(-1),
            device_id_type=MESH,
        )

    def ring_wait(array, side, step):
        index = tile(-step if side == 0 else step, core)
        pltpu.make_async_remote_copy(
            src_ref=landing(array, index),
            dst_ref=landing(array, index),
            send_sem=ring_send.at[array, side, step - 1],
            recv_sem=ring_recv.at[array, side, step - 1],
            device_id=device(1),
            device_id_type=MESH,
        ).wait_recv()

    def pair_copy(array, step, which):
        number = step % count
        index = tile(step, which)
        src = origin(array) if step == 0 else landing(array, index)
        return pltpu.make_async_remote_copy(
            src_ref=src,
            dst_ref=landing(array, index),
            send_sem=pair_send.at[array, number],
            recv_sem=pair_recv.at[array, number],
            device_id=partner,
            device_id_type=MESH,
        )

    def reach(array, side):
        return half if (array % 2) == side else half - 1

    bricks = targets[1].shape[0] - 1
    mine = (gx * chips_z + z) * slots
    targets[0][gx * chips_z + z] = sources[0][0]
    for number in (1, 2):
        targets[number][pl.ds(mine, slots)] = sources[number][...]
        targets[number][bricks] = jnp.zeros((rows, channels), jnp.bfloat16)
    pl.semaphore_wait(barrier, 3)
    started = []
    for step in range(1, half + 2):
        for array in range(5):
            for side in (0, 1):
                if step - 1 > reach(array, side):
                    continue
                if step > 1:
                    ring_wait(array, side, step - 1)
                if step <= reach(array, side):
                    copy = ring_copy(array, side, step)
                    copy.start()
                    started.append(copy)
                if step > 1:
                    copy = pair_copy(array, (1 - step) if side == 0 else (step - 1), core)
                    copy.start()
                    started.append(copy)
            if step == 1:
                copy = pair_copy(array, 0, core)
                copy.start()
                started.append(copy)
    for array in range(5):
        for number in range(count):
            pair_copy(array, number, 1 - core).wait_recv()
    for copy in started:
        copy.wait_send()


def gather_tiles(table, cot, features, chips_y, chips_z):
    count = chips_y * chips_z
    tiles = 2 * count
    padded = (tiles * slots + 1, rows, channels)
    whole = pl.BlockSpec(memory_space=pltpu.VMEM)
    return pl.pallas_call(
        functools.partial(gather_kernel, chips_y, chips_z),
        out_shape=[
            jax.ShapeDtypeStruct((tiles, 1, 128), jnp.int32),
            pltpu.VMEM(padded, jnp.bfloat16),
            pltpu.VMEM(padded, jnp.bfloat16),
        ],
        in_specs=[whole] * 3,
        out_specs=[whole] * 3,
        scratch_shapes=[
            pltpu.SemaphoreType.DMA((5, 2, count // 2)),
            pltpu.SemaphoreType.DMA((5, 2, count // 2)),
            pltpu.SemaphoreType.DMA((5, count)),
            pltpu.SemaphoreType.DMA((5, count)),
        ],
        compiler_params=pltpu.CompilerParams(
            collective_id=0, has_side_effects=True, vmem_limit_bytes=12 * 2**20
        ),
        name="gather_tiles",
    )(table, cot, features)


def conv_kernel(bricks, part_rows, picked, gy_size, *refs):
    (table, shifts, cot, feat, weight_hbm, out_ref, grad_ref, term_hbm) = refs[:8]
    (weight, near, total, flat, order, sems) = refs[8:]
    gx = lax.axis_index("gx")
    gy = lax.axis_index("gy")
    weight_copy = pltpu.make_async_copy(weight_hbm, weight, sems.at[0])
    weight_copy.start()
    total[...] = jnp.zeros_like(total)

    def entry(brick, offset):
        return table[brick // slots, (brick % slots) * 32 + offset]

    def count_live(brick, found):
        @pl.when(entry(brick, 13) != bricks)
        def _():
            order[found] = brick

        return found + (entry(brick, 13) != bricks).astype(jnp.int32)

    live = lax.fori_loop(0, bricks, count_live, jnp.int32(0))
    for extra in range(slots):
        order[live + extra] = 0

    def surround(source, slot, brick, valid, both):
        names = []
        for offset in range(27):
            name = entry(brick, offset)
            names.append(name if valid is None else jnp.where(valid, name, bricks))
        def move(side, plane, x):
            stack = jnp.concatenate(
                [source[side[n], pl.ds(plane, 16), :] for n in range(9)], axis=0
            )
            moved = jnp.dot(shifts[...], stack, preferred_element_type=jnp.float32)
            near[:, slot, x] = moved.astype(jnp.bfloat16).reshape(9, 16, channels)

        for x in range(4):
            move(names[9:18], x * 16, x + 1)
        if both:
            move(names[:9], 48, 0)
            move(names[18:], 0, 5)
        else:
            outer = [jnp.where(behind, names[n], names[18 + n]) for n in range(9)]
            plane = pl.multiple_of(jnp.where(behind, 48, 0), 16)
            move(outer, plane, jnp.where(behind, 0, 5))

    def window(a, b, c):
        return near[(b + 1) * 3 + c + 1, :, pl.ds(1 + a, 4)].reshape(slots * rows, channels)

    first = (gx * part_rows) // channels
    last = jnp.minimum(first + picked - 1, 26)
    behind = last // 9 == 2

    def group(number, carry):
        names = []
        for slot in range(slots):
            place = number * slots + slot
            brick = order[place]
            valid = place < live
            surround(cot, slot, brick, valid, False)
            names.append(brick)
        block = jnp.concatenate([feat[name] for name in names], axis=0).T

        def one(n, inner):
            offset = jnp.minimum(first + n, 26)
            a = offset // 9 - 1
            b = (offset // 3) % 3 - 1
            c = offset % 3 - 1
            at = pl.multiple_of(n * channels, channels)
            total[pl.ds(at, channels), :] += jnp.dot(
                block, window(-a, -b, -c), preferred_element_type=jnp.float32
            )
            return inner

        return lax.fori_loop(0, picked, one, carry, unroll=True)

    lax.fori_loop(0, (live + slots - 1) // slots, group, 0)
    start = pl.multiple_of(gx * part_rows - first * channels, 8)
    span = pl.ds(start, part_rows)
    total[span, :] = total[span, :] * kernel_scale
    result = pltpu.make_async_copy(total.at[span], term_hbm, sems.at[1])
    result.start()
    weight_copy.wait()
    mine = (gx * gy_size + gy) * slots
    for sign, source, target in ((-1, cot, grad_ref), (1, feat, out_ref)):
        for slot in range(slots):
            surround(source, slot, mine + slot, None, True)
        for offset in range(27):
            a, b, c = offset // 9 - 1, (offset // 3) % 3 - 1, offset % 3 - 1
            dims = (((1,), (0 if sign == 1 else 1,)), ((), ()))
            product = lax.dot_general(
                window(sign * a, sign * b, sign * c),
                weight[offset],
                dims,
                preferred_element_type=jnp.float32,
            )
            if offset == 0:
                flat[...] = product
            elif offset < 26:
                flat[...] += product
            else:
                target[...] = (flat[...] + product).astype(jnp.bfloat16)
    result.wait()


def convolve(table_all, cot_all, feat_all, kernel_weight, part_rows, picked, gy_size):
    bricks = cot_all.shape[0] - 1
    own = (slots * rows, channels)
    whole = pl.BlockSpec(memory_space=pltpu.VMEM)
    far = pl.BlockSpec(memory_space=pltpu.HBM)
    return pl.pallas_call(
        functools.partial(conv_kernel, bricks, part_rows, picked, gy_size),
        out_shape=[
            jax.ShapeDtypeStruct(own, jnp.bfloat16),
            jax.ShapeDtypeStruct(own, jnp.bfloat16),
            jax.ShapeDtypeStruct((part_rows, channels), jnp.float32),
        ],
        in_specs=[pl.BlockSpec(memory_space=pltpu.SMEM), whole, whole, whole, far],
        out_specs=[whole, whole, far],
        scratch_shapes=[
            pltpu.VMEM(kernel_weight.shape, jnp.bfloat16),
            pltpu.VMEM((9, slots, 6, 16, channels), jnp.bfloat16),
            pltpu.VMEM((picked * channels, channels), jnp.float32),
            pltpu.VMEM(own, jnp.float32),
            pltpu.SMEM((bricks + slots,), jnp.int32),
            pltpu.SemaphoreType.DMA((2,)),
        ],
        compiler_params=pltpu.CompilerParams(vmem_limit_bytes=16 * 2**20),
        name="convolve",
    )(table_all, shift_matrix(), cot_all, feat_all, kernel_weight)


def body(gx_size, gy_size, features, neighbour_table, kernel_weight, out_cotangent):
    gx = lax.axis_index("gx")
    gy = lax.axis_index("gy")
    tiles = gx_size * gy_size
    bricks = tiles * slots
    table = neighbour_table[0, 0]
    block = table // slots
    owner = (gx + block // 3 - 1) * gy_size + gy + block % 3 - 1
    named = jnp.where(table == 9 * slots, bricks, owner * slots + table % slots)
    named = jnp.pad(named, ((0, 0), (0, 5))).reshape(1, 1, 128)
    flat = (slots, rows, channels)
    table_all, cot_all, feat_all = gather_tiles(
        named, out_cotangent.reshape(flat), features.reshape(flat), gx_size // 2, gy_size
    )
    part_rows = 27 * channels // gx_size
    picked = max(
        -(-((g + 1) * part_rows) // channels) - g * part_rows // channels for g in range(gx_size)
    )
    out, grad, term = convolve(
        table_all.reshape(tiles, 128),
        cot_all,
        feat_all,
        kernel_weight,
        part_rows,
        picked,
        gy_size,
    )
    return out.reshape(features.shape), grad.reshape(features.shape), term


def solution(mesh):
    in_specs = (
        P(("groups", "gx"), "gy", None, None, None),
        P(("groups", "gx"), "gy", None, None),
        P(),
        P(("groups", "gx"), "gy", None, None, None),
    )
    out_specs = (
        P(("groups", "gx"), "gy", None, None, None),
        P(("groups", "gx"), "gy", None, None, None),
        P(("groups", "gx"), None),
    )
    return jax.shard_map(
        functools.partial(body, mesh.shape["gx"], mesh.shape["gy"]),
        mesh=mesh,
        in_specs=in_specs,
        out_specs=out_specs,
        check_vma=False,
    )
```

```python
import functools

import jax
import jax.numpy as jnp
import numpy as np
from jax import lax
from jax.experimental import pallas as pl
from jax.experimental.pallas import tpu as pltpu
from jax.sharding import PartitionSpec as P

kernel_scale = 0.00390625
slots = 4
rows = 64
channels = 256
MESH = pl.DeviceIdType.MESH


def shift_matrix():
    out = np.zeros((9, 4, 4, 9, 4, 4), np.float32)
    for b in (-1, 0, 1):
        for c in (-1, 0, 1):
            for y in range(4):
                for z in range(4):
                    source = ((y + b) // 4 + 1) * 3 + (z + c) // 4 + 1
                    out[(b + 1) * 3 + c + 1, y, z, source, (y + b) % 4, (z + c) % 4] = 1
    return jnp.asarray(out.reshape(144, 144), jnp.bfloat16)


def ring_place(position, chips_y, chips_z):
    inner = chips_y * (chips_z - 1)
    y_in = position // (chips_z - 1)
    step = position % (chips_z - 1)
    z_in = jnp.where(y_in % 2 == 0, 1 + step, chips_z - 1 - step)
    on_edge = position >= inner
    y = jnp.where(on_edge, chips_y - 1 - (position - inner), y_in)
    z = jnp.where(on_edge, 0, z_in)
    return y, z


def ring_position(y, z, chips_y, chips_z):
    inside = y * (chips_z - 1) + jnp.where(y % 2 == 0, z - 1, chips_z - 1 - z)
    return jnp.where(z == 0, chips_y * (chips_z - 1) + chips_y - 1 - y, inside)


def gather_kernel(chips_y, chips_z, *refs):
    sources = refs[0:3]
    targets = refs[3:6]
    own_sem, ring_send, ring_recv, pair_send, pair_recv = refs[6:]
    count = chips_y * chips_z
    half = count // 2
    gx = lax.axis_index("gx")
    z = lax.axis_index("gy")
    y = gx // 2
    core = gx % 2
    here = ring_position(y, z, chips_y, chips_z)

    def place(step):
        return ring_place((here + step + count) % count, chips_y, chips_z)

    def landing(stream, index):
        if stream == 0:
            return targets[0].at[index]
        return targets[(stream + 1) // 2].at[pl.ds(index * slots + (stream + 1) % 2 * 2, 2)]

    def origin(stream):
        if stream == 0:
            return sources[0].at[0]
        return sources[(stream + 1) // 2].at[pl.ds((stream + 1) % 2 * 2, 2)]

    def tile(step, which):
        ty, tz = place(step)
        return (ty * 2 + which) * chips_z + tz

    def device(step):
        ty, tz = place(step)
        return {"gx": ty * 2 + core, "gy": tz}

    partner = {"gx": y * 2 + 1 - core, "gy": z}
    near = (device(1), device(-1), partner)
    barrier = pltpu.get_barrier_semaphore()
    for peer in near:
        pl.semaphore_signal(barrier, inc=1, device_id=peer, device_id_type=MESH)

    def ring_copy(array, side, step):
        index = tile((1 - step) if side == 0 else (step - 1), core)
        src = origin(array) if step == 1 else landing(array, index)
        return pltpu.make_async_remote_copy(
            src_ref=src,
            dst_ref=landing(array, index),
            send_sem=ring_send.at[array, side, step - 1],
            recv_sem=ring_recv.at[array, side, step - 1],
            device_id=device(1) if side == 0 else device(-1),
            device_id_type=MESH,
        )

    def ring_wait(array, side, step):
        index = tile(-step if side == 0 else step, core)
        pltpu.make_async_remote_copy(
            src_ref=landing(array, index),
            dst_ref=landing(array, index),
            send_sem=ring_send.at[array, side, step - 1],
            recv_sem=ring_recv.at[array, side, step - 1],
            device_id=device(1),
            device_id_type=MESH,
        ).wait_recv()

    def pair_copy(array, step, which):
        number = step % count
        index = tile(step, which)
        src = origin(array) if step == 0 else landing(array, index)
        return pltpu.make_async_remote_copy(
            src_ref=src,
            dst_ref=landing(array, index),
            send_sem=pair_send.at[array, number],
            recv_sem=pair_recv.at[array, number],
            device_id=partner,
            device_id_type=MESH,
        )

    def reach(array, side):
        return half if (array % 2) == side else half - 1

    bricks = targets[1].shape[0] - 1
    mine = (gx * chips_z + z) * slots
    targets[0][gx * chips_z + z] = sources[0][0]
    own = []
    for number in (1, 2):
        copy = pltpu.make_async_copy(
            sources[number], targets[number].at[pl.ds(mine, slots)], own_sem.at[number - 1]
        )
        copy.start()
        own.append(copy)
        targets[number][bricks] = jnp.zeros((rows, channels), jnp.bfloat16)
    pl.semaphore_wait(barrier, 3)
    started = []
    for step in range(1, half + 2):
        for array in range(5):
            for side in (0, 1):
                if step - 1 > reach(array, side):
                    continue
                if step > 1:
                    ring_wait(array, side, step - 1)
                if step <= reach(array, side):
                    copy = ring_copy(array, side, step)
                    copy.start()
                    started.append(copy)
                if step > 1:
                    copy = pair_copy(array, (1 - step) if side == 0 else (step - 1), core)
                    copy.start()
                    started.append(copy)
            if step == 1:
                copy = pair_copy(array, 0, core)
                copy.start()
                started.append(copy)
    for array in range(5):
        for number in range(count):
            pair_copy(array, number, 1 - core).wait_recv()
    for copy in own:
        copy.wait()
    for copy in started:
        copy.wait_send()


def keep_far(array):
    return pltpu.with_memory_space_constraint(array, pltpu.HBM)


def gather_tiles(table, cot, features, chips_y, chips_z):
    count = chips_y * chips_z
    tiles = 2 * count
    padded = (tiles * slots + 1, rows, channels)
    whole = pl.BlockSpec(memory_space=pltpu.VMEM)
    return pl.pallas_call(
        functools.partial(gather_kernel, chips_y, chips_z),
        out_shape=[
            jax.ShapeDtypeStruct((tiles, 1, 128), jnp.int32),
            pltpu.VMEM(padded, jnp.bfloat16),
            pltpu.VMEM(padded, jnp.bfloat16),
        ],
        in_specs=[whole, pl.BlockSpec(memory_space=pltpu.HBM), pl.BlockSpec(memory_space=pltpu.HBM)],
        out_specs=[whole] * 3,
        scratch_shapes=[
            pltpu.SemaphoreType.DMA((2,)),
            pltpu.SemaphoreType.DMA((5, 2, count // 2)),
            pltpu.SemaphoreType.DMA((5, 2, count // 2)),
            pltpu.SemaphoreType.DMA((5, count)),
            pltpu.SemaphoreType.DMA((5, count)),
        ],
        compiler_params=pltpu.CompilerParams(
            collective_id=0, has_side_effects=True, vmem_limit_bytes=12 * 2**20
        ),
        name="gather_tiles",
    )(table, keep_far(cot), keep_far(features))


def conv_kernel(bricks, part_rows, picked, gy_size, *refs):
    (table, shift_hbm, cot, feat, weight_hbm, out_ref, grad_ref, term_hbm) = refs[:8]
    (shifts, weight, near, total, flat, order, sems) = refs[8:]
    gx = lax.axis_index("gx")
    gy = lax.axis_index("gy")
    shift_copy = pltpu.make_async_copy(shift_hbm, shifts, sems.at[2])
    shift_copy.start()
    weight_copy = pltpu.make_async_copy(weight_hbm, weight, sems.at[0])
    weight_copy.start()
    total[...] = jnp.zeros_like(total)

    def entry(brick, offset):
        return table[brick // slots, (brick % slots) * 32 + offset]

    def count_live(brick, found):
        @pl.when(entry(brick, 13) != bricks)
        def _():
            order[found] = brick

        return found + (entry(brick, 13) != bricks).astype(jnp.int32)

    live = lax.fori_loop(0, bricks, count_live, jnp.int32(0))
    for extra in range(slots):
        order[live + extra] = 0

    def surround(source, slot, brick, valid, both):
        names = []
        for offset in range(27):
            name = entry(brick, offset)
            names.append(name if valid is None else jnp.where(valid, name, bricks))
        def move(side, plane, x):
            stack = jnp.concatenate(
                [source[side[n], pl.ds(plane, 16), :] for n in range(9)], axis=0
            )
            moved = jnp.dot(shifts[...], stack, preferred_element_type=jnp.float32)
            near[:, slot, x] = moved.astype(jnp.bfloat16).reshape(9, 16, channels)

        for x in range(4):
            move(names[9:18], x * 16, x + 1)
        if both:
            move(names[:9], 48, 0)
            move(names[18:], 0, 5)
        else:
            outer = [jnp.where(behind, names[n], names[18 + n]) for n in range(9)]
            plane = pl.multiple_of(jnp.where(behind, 48, 0), 16)
            move(outer, plane, jnp.where(behind, 0, 5))

    def window(a, b, c):
        return near[(b + 1) * 3 + c + 1, :, pl.ds(1 + a, 4)].reshape(slots * rows, channels)

    shift_copy.wait()
    first = (gx * part_rows) // channels
    last = jnp.minimum(first + picked - 1, 26)
    behind = last // 9 == 2

    def group(number, carry):
        names = []
        for slot in range(slots):
            place = number * slots + slot
            brick = order[place]
            valid = place < live
            surround(cot, slot, brick, valid, False)
            names.append(brick)
        block = jnp.concatenate([feat[name] for name in names], axis=0).T

        def one(n, inner):
            offset = jnp.minimum(first + n, 26)
            a = offset // 9 - 1
            b = (offset // 3) % 3 - 1
            c = offset % 3 - 1
            at = pl.multiple_of(n * channels, channels)
            total[pl.ds(at, channels), :] += jnp.dot(
                block, window(-a, -b, -c), preferred_element_type=jnp.float32
            )
            return inner

        return lax.fori_loop(0, picked, one, carry, unroll=True)

    lax.fori_loop(0, (live + slots - 1) // slots, group, 0)
    start = pl.multiple_of(gx * part_rows - first * channels, 8)
    span = pl.ds(start, part_rows)
    total[span, :] = total[span, :] * kernel_scale
    result = pltpu.make_async_copy(total.at[span], term_hbm, sems.at[1])
    result.start()
    weight_copy.wait()
    mine = (gx * gy_size + gy) * slots
    for sign, source, target in ((-1, cot, grad_ref), (1, feat, out_ref)):
        for slot in range(slots):
            surround(source, slot, mine + slot, None, True)
        for offset in range(27):
            a, b, c = offset // 9 - 1, (offset // 3) % 3 - 1, offset % 3 - 1
            dims = (((1,), (0 if sign == 1 else 1,)), ((), ()))
            product = lax.dot_general(
                window(sign * a, sign * b, sign * c),
                weight[offset],
                dims,
                preferred_element_type=jnp.float32,
            )
            if offset == 0:
                flat[...] = product
            elif offset < 26:
                flat[...] += product
            else:
                target[...] = (flat[...] + product).astype(jnp.bfloat16)
    result.wait()


def convolve(table_all, cot_all, feat_all, kernel_weight, part_rows, picked, gy_size):
    bricks = cot_all.shape[0] - 1
    own = (slots * rows, channels)
    whole = pl.BlockSpec(memory_space=pltpu.VMEM)
    far = pl.BlockSpec(memory_space=pltpu.HBM)
    return pl.pallas_call(
        functools.partial(conv_kernel, bricks, part_rows, picked, gy_size),
        out_shape=[
            jax.ShapeDtypeStruct(own, jnp.bfloat16),
            jax.ShapeDtypeStruct(own, jnp.bfloat16),
            jax.ShapeDtypeStruct((part_rows, channels), jnp.float32),
        ],
        in_specs=[pl.BlockSpec(memory_space=pltpu.SMEM), far, whole, whole, far],
        out_specs=[whole, whole, far],
        scratch_shapes=[
            pltpu.VMEM((144, 144), jnp.bfloat16),
            pltpu.VMEM(kernel_weight.shape, jnp.bfloat16),
            pltpu.VMEM((9, slots, 6, 16, channels), jnp.bfloat16),
            pltpu.VMEM((picked * channels, channels), jnp.float32),
            pltpu.VMEM(own, jnp.float32),
            pltpu.SMEM((bricks + slots,), jnp.int32),
            pltpu.SemaphoreType.DMA((3,)),
        ],
        compiler_params=pltpu.CompilerParams(vmem_limit_bytes=16 * 2**20),
        name="convolve",
    )(table_all, keep_far(shift_matrix()), cot_all, feat_all, keep_far(kernel_weight))


def body(gx_size, gy_size, features, neighbour_table, kernel_weight, out_cotangent):
    gx = lax.axis_index("gx")
    gy = lax.axis_index("gy")
    tiles = gx_size * gy_size
    bricks = tiles * slots
    table = neighbour_table[0, 0]
    block = table // slots
    owner = (gx + block // 3 - 1) * gy_size + gy + block % 3 - 1
    named = jnp.where(table == 9 * slots, bricks, owner * slots + table % slots)
    named = jnp.pad(named, ((0, 0), (0, 5))).reshape(1, 1, 128)
    flat = (slots, rows, channels)
    table_all, cot_all, feat_all = gather_tiles(
        named, out_cotangent.reshape(flat), features.reshape(flat), gx_size // 2, gy_size
    )
    part_rows = 27 * channels // gx_size
    picked = max(
        -(-((g + 1) * part_rows) // channels) - g * part_rows // channels for g in range(gx_size)
    )
    out, grad, term = convolve(
        table_all.reshape(tiles, 128),
        cot_all,
        feat_all,
        kernel_weight,
        part_rows,
        picked,
        gy_size,
    )
    return out.reshape(features.shape), grad.reshape(features.shape), term


def solution(mesh):
    in_specs = (
        P(("groups", "gx"), "gy", None, None, None),
        P(("groups", "gx"), "gy", None, None),
        P(),
        P(("groups", "gx"), "gy", None, None, None),
    )
    out_specs = (
        P(("groups", "gx"), "gy", None, None, None),
        P(("groups", "gx"), "gy", None, None, None),
        P(("groups", "gx"), None),
    )
    return jax.shard_map(
        functools.partial(body, mesh.shape["gx"], mesh.shape["gy"]),
        mesh=mesh,
        in_specs=in_specs,
        out_specs=out_specs,
        check_vma=False,
    )
```

```python
import functools

import jax
import jax.numpy as jnp
import numpy as np
from jax import lax
from jax.experimental import pallas as pl
from jax.experimental.pallas import tpu as pltpu
from jax.sharding import PartitionSpec as P

kernel_scale = 0.00390625
slots = 4
rows = 64
channels = 256
MESH = pl.DeviceIdType.MESH


def shift_matrix():
    out = np.zeros((9, 4, 4, 9, 4, 4), np.float32)
    for b in (-1, 0, 1):
        for c in (-1, 0, 1):
            for y in range(4):
                for z in range(4):
                    source = ((y + b) // 4 + 1) * 3 + (z + c) // 4 + 1
                    out[(b + 1) * 3 + c + 1, y, z, source, (y + b) % 4, (z + c) % 4] = 1
    return jnp.asarray(out.reshape(144, 144), jnp.bfloat16)


def ring_place(position, chips_y, chips_z):
    inner = chips_y * (chips_z - 1)
    y_in = position // (chips_z - 1)
    step = position % (chips_z - 1)
    z_in = jnp.where(y_in % 2 == 0, 1 + step, chips_z - 1 - step)
    on_edge = position >= inner
    y = jnp.where(on_edge, chips_y - 1 - (position - inner), y_in)
    z = jnp.where(on_edge, 0, z_in)
    return y, z


def ring_position(y, z, chips_y, chips_z):
    inside = y * (chips_z - 1) + jnp.where(y % 2 == 0, z - 1, chips_z - 1 - z)
    return jnp.where(z == 0, chips_y * (chips_z - 1) + chips_y - 1 - y, inside)


def gather_kernel(chips_y, chips_z, *refs):
    sources = refs[0:3]
    table, shift_hbm, weight_hbm = refs[3:6]
    targets = refs[6:9]
    grad_ref, shifts, weight, near, flat = refs[9:14]
    own_sem, ring_send, ring_recv, pair_send, pair_recv = refs[14:]
    loads = (
        pltpu.make_async_copy(shift_hbm, shifts, own_sem.at[2]),
        pltpu.make_async_copy(weight_hbm, weight, own_sem.at[3]),
    )
    for load in loads:
        load.start()
    count = chips_y * chips_z
    half = count // 2
    gx = lax.axis_index("gx")
    z = lax.axis_index("gy")
    y = gx // 2
    core = gx % 2
    here = ring_position(y, z, chips_y, chips_z)

    def place(step):
        return ring_place((here + step + count) % count, chips_y, chips_z)

    def landing(stream, index):
        if stream == 0:
            return targets[0].at[index]
        return targets[(stream + 1) // 2].at[pl.ds(index * slots + (stream + 1) % 2 * 2, 2)]

    def origin(stream):
        if stream == 0:
            return sources[0].at[0]
        return sources[(stream + 1) // 2].at[pl.ds((stream + 1) % 2 * 2, 2)]

    def tile(step, which):
        ty, tz = place(step)
        return (ty * 2 + which) * chips_z + tz

    def device(step):
        ty, tz = place(step)
        return {"gx": ty * 2 + core, "gy": tz}

    partner = {"gx": y * 2 + 1 - core, "gy": z}
    peers = (device(1), device(-1), partner)
    barrier = pltpu.get_barrier_semaphore()
    for peer in peers:
        pl.semaphore_signal(barrier, inc=1, device_id=peer, device_id_type=MESH)

    def ring_copy(array, side, step):
        index = tile((1 - step) if side == 0 else (step - 1), core)
        src = origin(array) if step == 1 else landing(array, index)
        return pltpu.make_async_remote_copy(
            src_ref=src,
            dst_ref=landing(array, index),
            send_sem=ring_send.at[array, side, step - 1],
            recv_sem=ring_recv.at[array, side, step - 1],
            device_id=device(1) if side == 0 else device(-1),
            device_id_type=MESH,
        )

    def ring_wait(array, side, step):
        index = tile(-step if side == 0 else step, core)
        pltpu.make_async_remote_copy(
            src_ref=landing(array, index),
            dst_ref=landing(array, index),
            send_sem=ring_send.at[array, side, step - 1],
            recv_sem=ring_recv.at[array, side, step - 1],
            device_id=device(1),
            device_id_type=MESH,
        ).wait_recv()

    def pair_copy(array, step, which):
        number = step % count
        index = tile(step, which)
        src = origin(array) if step == 0 else landing(array, index)
        return pltpu.make_async_remote_copy(
            src_ref=src,
            dst_ref=landing(array, index),
            send_sem=pair_send.at[array, number],
            recv_sem=pair_recv.at[array, number],
            device_id=partner,
            device_id_type=MESH,
        )

    def reach(array, side):
        return half if (array % 2) == side else half - 1

    bricks = targets[1].shape[0] - 1
    mine = (gx * chips_z + z) * slots
    targets[0][gx * chips_z + z] = sources[0][0]
    own = []
    for number in (1, 2):
        copy = pltpu.make_async_copy(
            sources[number], targets[number].at[pl.ds(mine, slots)], own_sem.at[number - 1]
        )
        copy.start()
        own.append(copy)
        targets[number][bricks] = jnp.zeros((rows, channels), jnp.bfloat16)
    pl.semaphore_wait(barrier, 3)
    started = []
    def launch(copy):
        copy.start()
        started.append(copy)

    def advance(streams, step):
        for stream in streams:
            for side in (0, 1):
                if step - 1 > reach(stream, side):
                    continue
                if step > 1:
                    ring_wait(stream, side, step - 1)
                if step <= reach(stream, side):
                    launch(ring_copy(stream, side, step))
                if step > 1:
                    launch(pair_copy(stream, (1 - step) if side == 0 else (step - 1), core))
            if step == 1:
                launch(pair_copy(stream, 0, core))

    def settle(streams):
        for stream in streams:
            for number in range(count):
                pair_copy(stream, number, 1 - core).wait_recv()

    early, late = (0, 1, 2), (3, 4)
    for step in range(1, half + 1):
        advance(early, step)
    advance(late, 1)
    advance(early, half + 1)
    settle(early)
    for copy in own + list(loads):
        copy.wait()
    cot = targets[1]

    def own_slot(slot, carry):
        names = [table[0, slot * 32 + offset] for offset in range(27)]
        for x in range(6):
            side = (x + 3) // 4
            plane = (x + 3) % 4 * 16
            stack = jnp.concatenate(
                [cot[names[side * 9 + n], plane : plane + 16, :] for n in range(9)], axis=0
            )
            moved = jnp.dot(shifts[...], stack, preferred_element_type=jnp.float32)
            near[:, slot, x] = moved.astype(jnp.bfloat16).reshape(9, 16, channels)
        return carry

    def pull(bc, carry):
        for a in range(3):
            seen = near[8 - bc, :, 2 - a : 6 - a].reshape(slots * rows, channels)
            flat[...] += lax.dot_general(
                seen,
                weight[a * 9 + bc],
                (((1,), (1,)), ((), ())),
                preferred_element_type=jnp.float32,
            )
        return carry

    flat[...] = jnp.zeros_like(flat)
    lax.fori_loop(0, slots, own_slot, 0)
    for step in range(2, half + 2):
        advance(late, step)
        low = 9 * (step - 2) // half
        high = 9 * (step - 1) // half
        lax.fori_loop(low, high, pull, 0)
    grad_ref[...] = flat[...].astype(jnp.bfloat16)
    settle(late)
    for copy in started:
        copy.wait_send()


def keep_far(array):
    return pltpu.with_memory_space_constraint(array, pltpu.HBM)


def gather_tiles(table, cot, features, kernel_weight, chips_y, chips_z):
    count = chips_y * chips_z
    tiles = 2 * count
    far = pl.BlockSpec(memory_space=pltpu.HBM)
    padded = (tiles * slots + 1, rows, channels)
    whole = pl.BlockSpec(memory_space=pltpu.VMEM)
    return pl.pallas_call(
        functools.partial(gather_kernel, chips_y, chips_z),
        out_shape=[
            jax.ShapeDtypeStruct((tiles, 1, 128), jnp.int32),
            pltpu.VMEM(padded, jnp.bfloat16),
            pltpu.VMEM(padded, jnp.bfloat16),
            pltpu.VMEM((slots * rows, channels), jnp.bfloat16),
        ],
        in_specs=[whole, far, far, pl.BlockSpec(memory_space=pltpu.SMEM), far, far],
        out_specs=[whole] * 4,
        scratch_shapes=[
            pltpu.VMEM((144, 144), jnp.bfloat16),
            pltpu.VMEM(kernel_weight.shape, jnp.bfloat16),
            pltpu.VMEM((9, slots, 6, 16, channels), jnp.bfloat16),
            pltpu.VMEM((slots * rows, channels), jnp.float32),
            pltpu.SemaphoreType.DMA((4,)),
            pltpu.SemaphoreType.DMA((5, 2, count // 2)),
            pltpu.SemaphoreType.DMA((5, 2, count // 2)),
            pltpu.SemaphoreType.DMA((5, count)),
            pltpu.SemaphoreType.DMA((5, count)),
        ],
        compiler_params=pltpu.CompilerParams(
            collective_id=0, has_side_effects=True, vmem_limit_bytes=12 * 2**20
        ),
        name="gather_tiles",
    )(
        table,
        keep_far(cot),
        keep_far(features),
        table.reshape(1, 128),
        keep_far(shift_matrix()),
        keep_far(kernel_weight),
    )


def conv_kernel(bricks, part_rows, picked, gy_size, *refs):
    (table, shift_hbm, cot, feat, weight_hbm, pulled, out_ref, grad_ref, term_hbm) = refs[:9]
    (shifts, weight, near, total, flat, order, sems) = refs[9:]
    gx = lax.axis_index("gx")
    gy = lax.axis_index("gy")
    shift_copy = pltpu.make_async_copy(shift_hbm, shifts, sems.at[2])
    shift_copy.start()
    weight_copy = pltpu.make_async_copy(weight_hbm, weight, sems.at[0])
    weight_copy.start()
    total[...] = jnp.zeros_like(total)

    def entry(brick, offset):
        return table[brick // slots, (brick % slots) * 32 + offset]

    def count_live(brick, found):
        @pl.when(entry(brick, 13) != bricks)
        def _():
            order[found] = brick

        return found + (entry(brick, 13) != bricks).astype(jnp.int32)

    live = lax.fori_loop(0, bricks, count_live, jnp.int32(0))
    for extra in range(slots):
        order[live + extra] = 0

    def surround(source, slot, brick, valid, both):
        names = []
        for offset in range(27):
            name = entry(brick, offset)
            names.append(name if valid is None else jnp.where(valid, name, bricks))
        def move(side, plane, x):
            stack = jnp.concatenate(
                [source[side[n], pl.ds(plane, 16), :] for n in range(9)], axis=0
            )
            moved = jnp.dot(shifts[...], stack, preferred_element_type=jnp.float32)
            near[:, slot, x] = moved.astype(jnp.bfloat16).reshape(9, 16, channels)

        for x in range(4):
            move(names[9:18], x * 16, x + 1)
        if both:
            move(names[:9], 48, 0)
            move(names[18:], 0, 5)
        else:
            outer = [jnp.where(behind, names[n], names[18 + n]) for n in range(9)]
            plane = pl.multiple_of(jnp.where(behind, 48, 0), 16)
            move(outer, plane, jnp.where(behind, 0, 5))

    def window(a, b, c):
        return near[(b + 1) * 3 + c + 1, :, pl.ds(1 + a, 4)].reshape(slots * rows, channels)

    shift_copy.wait()
    first = (gx * part_rows) // channels
    last = jnp.minimum(first + picked - 1, 26)
    behind = last // 9 == 2

    def group(number, carry):
        names = []
        for slot in range(slots):
            place = number * slots + slot
            brick = order[place]
            valid = place < live
            surround(cot, slot, brick, valid, False)
            names.append(brick)
        block = jnp.concatenate([feat[name] for name in names], axis=0).T

        def one(n, inner):
            offset = jnp.minimum(first + n, 26)
            a = offset // 9 - 1
            b = (offset // 3) % 3 - 1
            c = offset % 3 - 1
            at = pl.multiple_of(n * channels, channels)
            total[pl.ds(at, channels), :] += jnp.dot(
                block, window(-a, -b, -c), preferred_element_type=jnp.float32
            )
            return inner

        return lax.fori_loop(0, picked, one, carry, unroll=True)

    lax.fori_loop(0, (live + slots - 1) // slots, group, 0)
    start = pl.multiple_of(gx * part_rows - first * channels, 8)
    span = pl.ds(start, part_rows)
    total[span, :] = total[span, :] * kernel_scale
    result = pltpu.make_async_copy(total.at[span], term_hbm, sems.at[1])
    result.start()
    weight_copy.wait()
    mine = (gx * gy_size + gy) * slots
    grad_ref[...] = pulled[...]
    for sign, source, target in ((1, feat, out_ref),):
        for slot in range(slots):
            surround(source, slot, mine + slot, None, True)
        for offset in range(27):
            a, b, c = offset // 9 - 1, (offset // 3) % 3 - 1, offset % 3 - 1
            dims = (((1,), (0 if sign == 1 else 1,)), ((), ()))
            product = lax.dot_general(
                window(sign * a, sign * b, sign * c),
                weight[offset],
                dims,
                preferred_element_type=jnp.float32,
            )
            if offset == 0:
                flat[...] = product
            elif offset < 26:
                flat[...] += product
            else:
                target[...] = (flat[...] + product).astype(jnp.bfloat16)
    result.wait()


def convolve(table_all, cot_all, feat_all, kernel_weight, pulled, part_rows, picked, gy_size):
    bricks = cot_all.shape[0] - 1
    own = (slots * rows, channels)
    whole = pl.BlockSpec(memory_space=pltpu.VMEM)
    far = pl.BlockSpec(memory_space=pltpu.HBM)
    return pl.pallas_call(
        functools.partial(conv_kernel, bricks, part_rows, picked, gy_size),
        out_shape=[
            jax.ShapeDtypeStruct(own, jnp.bfloat16),
            jax.ShapeDtypeStruct(own, jnp.bfloat16),
            jax.ShapeDtypeStruct((part_rows, channels), jnp.float32),
        ],
        in_specs=[pl.BlockSpec(memory_space=pltpu.SMEM), far, whole, whole, far, whole],
        out_specs=[whole, whole, far],
        scratch_shapes=[
            pltpu.VMEM((144, 144), jnp.bfloat16),
            pltpu.VMEM(kernel_weight.shape, jnp.bfloat16),
            pltpu.VMEM((9, slots, 6, 16, channels), jnp.bfloat16),
            pltpu.VMEM((picked * channels, channels), jnp.float32),
            pltpu.VMEM(own, jnp.float32),
            pltpu.SMEM((bricks + slots,), jnp.int32),
            pltpu.SemaphoreType.DMA((3,)),
        ],
        compiler_params=pltpu.CompilerParams(vmem_limit_bytes=16 * 2**20),
        name="convolve",
    )(table_all, keep_far(shift_matrix()), cot_all, feat_all, keep_far(kernel_weight), pulled)


def body(gx_size, gy_size, features, neighbour_table, kernel_weight, out_cotangent):
    gx = lax.axis_index("gx")
    gy = lax.axis_index("gy")
    tiles = gx_size * gy_size
    bricks = tiles * slots
    table = neighbour_table[0, 0]
    block = table // slots
    owner = (gx + block // 3 - 1) * gy_size + gy + block % 3 - 1
    named = jnp.where(table == 9 * slots, bricks, owner * slots + table % slots)
    named = jnp.pad(named, ((0, 0), (0, 5))).reshape(1, 1, 128)
    flat = (slots, rows, channels)
    table_all, cot_all, feat_all, pulled = gather_tiles(
        named, out_cotangent.reshape(flat), features.reshape(flat), kernel_weight, gx_size // 2, gy_size
    )
    part_rows = 27 * channels // gx_size
    picked = max(
        -(-((g + 1) * part_rows) // channels) - g * part_rows // channels for g in range(gx_size)
    )
    out, grad, term = convolve(
        table_all.reshape(tiles, 128),
        cot_all,
        feat_all,
        kernel_weight,
        pulled,
        part_rows,
        picked,
        gy_size,
    )
    return out.reshape(features.shape), grad.reshape(features.shape), term


def solution(mesh):
    in_specs = (
        P(("groups", "gx"), "gy", None, None, None),
        P(("groups", "gx"), "gy", None, None),
        P(),
        P(("groups", "gx"), "gy", None, None, None),
    )
    out_specs = (
        P(("groups", "gx"), "gy", None, None, None),
        P(("groups", "gx"), "gy", None, None, None),
        P(("groups", "gx"), None),
    )
    return jax.shard_map(
        functools.partial(body, mesh.shape["gx"], mesh.shape["gy"]),
        mesh=mesh,
        in_specs=in_specs,
        out_specs=out_specs,
        check_vma=False,
    )
```
